32 devices in a mesh: lat: 4 (over x, core), lon: 8 (over z, y).
Axes of the slice: x: 2, y: 2, z: 4, core: 2. Of those that a mesh axis runs over, the one named last changes fastest.
Arguments:
- tokens: bfloat16 [32, 1440, 512], P('lat', 'lon'), may hold values from -6 to 6
- ln_gain: float32 [512], replicated, may hold values from 0.25 to 1.75
- w_qkv: bfloat16 [512, 1536], replicated, may hold values from -6 to 6
- w_out: bfloat16 [512, 512], replicated, may hold values from -1 to 1
- zonal_slope: float32 [4], replicated, may hold values from 0.5 to 8
- merid_slope: float32 [4], replicated, may hold values from 0.5 to 8
Outputs:
- update: bfloat16 [32, 1440, 512], P('lat', 'lon')
The draws below stay inside these ranges and needn't reach their ends.
All inputs are finite; a program needn't handle non-finite values.
Results may differ from the reference program's by a relative error of at most 0.0084.
Values may be sent and summed in bfloat16 or wider, within the bound.
A program may use at most 128 MiB of HBM per device.

```python
import math
import jax
import jax.numpy as jnp
from jax import lax

D = 512
HEADS = 8
HD = 64
NLON = 1440
NLAT = 32


def draw_w_qkv(key, part):
    first, second, third = jax.random.split(key, 3)
    factor = D ** (-0.5)
    queries = jnp.clip(jax.random.normal(first, (D, D), jnp.float32), -4.0, 4.0) * factor
    keys = jnp.clip(jax.random.normal(second, (D, D), jnp.float32), -4.0, 4.0) * factor
    values = jnp.clip(jax.random.normal(third, (D, D), jnp.float32), -4.0, 4.0) * factor
    return jnp.concatenate([queries, keys, values], axis=1).astype(jnp.bfloat16)


def levels(key, dims, pieces, least, high):
    loudness, own = 1.0, jax.random.fold_in(key, 6)
    for dim, blocks in pieces:
        draws = jnp.exp(jax.random.uniform(jax.random.fold_in(own, dim), (blocks,), jnp.float32, least / len(pieces), high / len(pieces)))
        loudness = loudness * jnp.repeat(draws, dims[dim] // blocks).reshape([-1 if axis == dim else 1 for axis in range(len(dims))])
    return loudness


def noise(key, dims, width, bound, cuts=(), kind=jnp.bfloat16):
    level = levels(key, dims, cuts, -0.22, 0.18) if cuts else 1.0
    drawn = jax.random.normal(key, dims, jnp.float32) * width * level
    return jnp.minimum(jnp.maximum(drawn, -bound), bound).astype(kind)


def setup_inputs(seed: int = 0) -> dict:
    key_of = jax.random.split(jax.random.key(seed), 7)
    tokens = noise(key_of[0], (NLAT, NLON, D), 1.0, 6.0, ((0, 4), (1, 8)))
    ln_gain = jnp.clip(1.0 + 0.15 * jax.random.normal(key_of[1], (D,), jnp.float32), 0.25, 1.75)
    w_qkv = draw_w_qkv(jax.random.fold_in(key_of[6], 71), 0)
    w_out = noise(key_of[3], (D, D), (D // 16) ** -0.5, 1.0)
    zonal_slope = jnp.clip(jnp.exp(jax.random.uniform(key_of[4], (HEADS // 2,), jnp.float32, math.log(0.5), math.log(8.0))), 0.5, 8.0)
    merid_slope = jnp.clip(jnp.exp(jax.random.uniform(key_of[5], (HEADS // 2,), jnp.float32, math.log(0.5), math.log(8.0))), 0.5, 8.0)
    return {"tokens": tokens, "ln_gain": ln_gain, "w_qkv": w_qkv, "w_out": w_out, "zonal_slope": zonal_slope, "merid_slope": merid_slope}


def norm_rows(tokens, gain):
    values = tokens.astype(jnp.float32)
    center = values - lax.optimization_barrier(jnp.mean(values, axis=-1, keepdims=True))
    spread = lax.optimization_barrier(jnp.mean(center * center, axis=-1, keepdims=True))
    return (center * lax.rsqrt(spread + 1e-05) * gain).astype(jnp.bfloat16)

def attend_line(query, keys, values, bias):
    scores = jnp.einsum('qhd,khd->hqk', query.astype(jnp.float32), keys.astype(jnp.float32)) * HD ** (-0.5) + bias
    top = lax.optimization_barrier(jnp.max(scores, axis=-1, keepdims=True))
    weights = jnp.exp(scores - top)
    total = lax.optimization_barrier(jnp.sum(weights, axis=-1))
    rounded = lax.optimization_barrier(weights.astype(jnp.bfloat16))
    summed = jnp.einsum('hqk,khd->qhd', rounded.astype(jnp.float32), values.astype(jnp.float32))
    return summed / jnp.transpose(total)[:, :, None]

def reference(tokens, ln_gain, w_qkv, w_out, zonal_slope, merid_slope):
    half = HEADS // 2
    normed = norm_rows(tokens, ln_gain)
    qkv = jnp.dot(normed.reshape(NLAT * NLON, D), w_qkv, preferred_element_type=jnp.float32).astype(jnp.bfloat16)
    qkv = qkv.reshape(NLAT, NLON, 3, 2, half, HD)
    lon_pos = jnp.arange(NLON)
    lon_gap = jnp.abs(lon_pos[:, None] - lon_pos[None, :])
    circle = jnp.minimum(lon_gap, NLON - lon_gap).astype(jnp.float32) / NLON
    zonal_bias = -zonal_slope[:, None, None] * circle[None]
    zonal = lax.map(lambda row: attend_line(row[:, 0], row[:, 1], row[:, 2], zonal_bias), qkv[:, :, :, 0])
    lat_pos = jnp.arange(NLAT)
    lat_gap = jnp.abs(lat_pos[:, None] - lat_pos[None, :]).astype(jnp.float32) / NLAT
    merid_bias = -merid_slope[:, None, None] * lat_gap[None]
    columns = jnp.transpose(qkv[:, :, :, 1], (1, 0, 2, 3, 4))
    merid = lax.map(lambda col: attend_line(col[:, 0], col[:, 1], col[:, 2], merid_bias), columns)
    merid = jnp.transpose(merid, (1, 0, 2, 3))
    attended = jnp.concatenate([zonal.reshape(NLAT, NLON, half * HD), merid.reshape(NLAT, NLON, half * HD)], axis=-1)
    attended = attended.astype(jnp.bfloat16)
    update = jnp.dot(attended.reshape(NLAT * NLON, D), w_out, preferred_element_type=jnp.float32)
    return update.astype(jnp.bfloat16).reshape(NLAT, NLON, D)
```

```python
import functools
import math
import jax
import jax.numpy as jnp
from jax import lax
from jax.experimental import pallas as pl
from jax.experimental.pallas import tpu as pltpu
from jax.sharding import PartitionSpec as P

HEADS = 8
HD = 64
HALF = HEADS // 2
GW = HALF * HD
LOG2E = math.log2(math.e)
FAR = -1e30
BF = jnp.bfloat16
F32 = jnp.float32
MESH = pl.DeviceIdType.MESH

def norm_rows(tokens, gain):
    values = tokens.astype(jnp.float32)
    center = values - jnp.mean(values, axis=-1, keepdims=True)
    spread = jnp.mean(center * center, axis=-1, keepdims=True)
    return (center * lax.rsqrt(spread + 1e-05) * gain).astype(jnp.bfloat16)


def fold_step(carry, scores, values, form):
    top, total, summed = carry
    top_new = jnp.maximum(top, jnp.max(scores, axis=-1))
    weights = jnp.exp(scores - top_new[..., None])
    total = jnp.sum(weights, axis=-1)
    summed = jnp.einsum(
        form, weights.astype(jnp.bfloat16), values, preferred_element_type=jnp.float32
    )
    return (top_new, total, summed)


def gathered(tokens, ln_gain, w_qkv, w_out, zonal_slope, merid_slope):
    lat_rows, lon_cols, width = tokens.shape
    half = HEADS // 2
    scale = HD ** (-0.5)
    normed = norm_rows(tokens, ln_gain)
    qkv = jnp.dot(
        normed.reshape(lat_rows * lon_cols, width), w_qkv, preferred_element_type=jnp.float32
    ).astype(jnp.bfloat16)
    qkv = qkv.reshape(lat_rows, lon_cols, 3, 2, half, HD)
    lon_total = lon_cols * lax.axis_size("lon")
    lat_total = lat_rows * lax.axis_size("lat")
    zonal_query = qkv[:, :, 0, 0]
    zonal_pairs = qkv[:, :, 1:, 0]
    query_pos = lax.axis_index("lon") * lon_cols + jnp.arange(lon_cols, dtype=jnp.int32)
    start_carry = (
        jnp.full((lat_rows, half, lon_cols), -1e30, jnp.float32),
        jnp.zeros((lat_rows, half, lon_cols), jnp.float32),
        jnp.zeros((lat_rows, half, lon_cols, HD), jnp.float32),
    )
    piece = lax.all_gather(zonal_pairs, "lon", axis=1, tiled=True)
    count = piece.shape[1]
    key_pos = jnp.arange(count, dtype=jnp.int32)
    gap = jnp.abs(query_pos[:, None] - key_pos[None, :])
    circle = jnp.minimum(gap, lon_total - gap).astype(jnp.float32) / lon_total
    bias = -zonal_slope[:, None, None] * circle[None]
    scores = (
        jnp.einsum(
            "ajhd,akhd->ahjk", zonal_query, piece[:, :, 0], preferred_element_type=jnp.float32
        )
        * scale
        + bias[None]
    )
    top, total, summed = fold_step(start_carry, scores, piece[:, :, 1], "ahjk,akhd->ahjd")
    zonal = jnp.transpose(summed / total[..., None], (0, 2, 1, 3)).reshape(
        lat_rows, lon_cols, half * HD
    )
    merid_query = qkv[:, :, 0, 1]
    merid_pairs = qkv[:, :, 1:, 1]
    row_pos = lax.axis_index("lat") * lat_rows + jnp.arange(lat_rows, dtype=jnp.int32)
    start_carry = (
        jnp.full((lon_cols, half, lat_rows), -1e30, jnp.float32),
        jnp.zeros((lon_cols, half, lat_rows), jnp.float32),
        jnp.zeros((lon_cols, half, lat_rows, HD), jnp.float32),
    )
    piece = lax.all_gather(merid_pairs, "lat", axis=0, tiled=True)
    count = piece.shape[0]
    key_pos = jnp.arange(count, dtype=jnp.int32)
    gap = jnp.abs(row_pos[:, None] - key_pos[None, :]).astype(jnp.float32) / lat_total
    bias = -merid_slope[:, None, None] * gap[None]
    scores = (
        jnp.einsum(
            "ajhd,bjhd->jhab", merid_query, piece[:, :, 0], preferred_element_type=jnp.float32
        )
        * scale
        + bias[None]
    )
    top, total, summed = fold_step(start_carry, scores, piece[:, :, 1], "jhab,bjhd->jhad")
    merid = jnp.transpose(summed / total[..., None], (2, 0, 1, 3)).reshape(
        lat_rows, lon_cols, half * HD
    )
    attended = jnp.concatenate([zonal, merid], axis=-1).astype(jnp.bfloat16)
    update = jnp.dot(
        attended.reshape(lat_rows * lon_cols, width), w_out, preferred_element_type=jnp.float32
    )
    return update.astype(jnp.bfloat16).reshape(lat_rows, lon_cols, width)

def normed_of(x, gain):
    v = x.astype(F32)
    c = v - jnp.mean(v, axis=-1, keepdims=True)
    s = jnp.mean(c * c, axis=-1, keepdims=True)
    return (c * lax.rsqrt(s + 1e-05) * gain).astype(BF)


def mm(a, b):
    return jnp.dot(a, b, preferred_element_type=F32)


def mm_t(a, b):
    return lax.dot_general(a, b, (((1,), (1,)), ((), ())), preferred_element_type=F32)


def batch_of(n):
    return max(d for d in range(1, 6) if n % d == 0)


def kernel(dims, tok_ref, gain_ref, wqkv_ref, zs_ref, ms_ref, out_ref,
           flat, rowsrc, rowbuf, colbuf, qx, kx, vx, zbias, mbias, mqkv, s_ref, p_ref, o_ref,
           m_ref, al_ref, lt_ref, acc, den, ms_scr, mp_scr, ml_scr,
           zout, mout, zret, mret, zflat,
           zsend, zrecv, msend, mrecv, zrs, zrr, mrs, mrr):
    nlon, nlat, rows, cols, width = dims
    chunk = cols // nlat
    step = qx.shape[1] // nlon
    qb = 2 * step
    span = nlon * step
    lon_total = nlon * cols
    lat_total = nlat * rows
    pairs = HALF // 2
    me = lax.axis_index("lon")
    la = lax.axis_index("lat")
    zi = me // 2
    yi = lax.rem(me, 2)
    odd = lax.rem(zi + yi, 2)

    def bit(a, b):
        return a + b - 2 * a * b

    def block_of(slot):
        return 2 * bit(zi // 2, slot // 2) + bit(lax.rem(zi, 2), slot % 2)

    def peer(slot, flip):
        return 2 * block_of(slot) + bit(yi, flip)

    barrier = pltpu.get_barrier_semaphore()
    for k in range(1, nlon):
        pl.semaphore_signal(barrier, inc=1, device_id={"lon": lax.rem(me + k, nlon)}, device_id_type=MESH)
    for k in range(1, nlat):
        pl.semaphore_signal(barrier, inc=1, device_id={"lat": lax.rem(la + k, nlat)}, device_id_type=MESH)
    pl.semaphore_wait(barrier, nlon + nlat - 2)

    def zcopy(dst, src):
        return pltpu.make_async_remote_copy(
            src_ref=rowsrc.at[dst], dst_ref=rowbuf.at[src], send_sem=zsend.at[dst],
            recv_sem=zrecv.at[src], device_id={"lon": dst}, device_id_type=MESH)

    def mcopy(dst, src):
        return pltpu.make_async_remote_copy(
            src_ref=tok_ref.at[pl.ds(dst * chunk, chunk)],
            dst_ref=colbuf.at[src], send_sem=msend.at[dst],
            recv_sem=mrecv.at[src], device_id={"lat": dst}, device_id_type=MESH)

    def zback(dst, src):
        return pltpu.make_async_remote_copy(
            src_ref=zout.at[dst], dst_ref=zret.at[src], send_sem=zrs.at[dst],
            recv_sem=zrr.at[src], device_id={"lon": dst}, device_id_type=MESH)

    def mback(dst, src):
        return pltpu.make_async_remote_copy(
            src_ref=mout.at[dst],
            dst_ref=mret.at[pl.ds(src * chunk, chunk)], send_sem=mrs.at[dst],
            recv_sem=mrr.at[src], device_id={"lat": dst}, device_id_type=MESH)

    for k in range(1, nlat):
        mcopy(lax.rem(la + k, nlat), la).start()

    def flatten(i, _):
        part = tok_ref[pl.ds(i * chunk, chunk)].astype(F32).reshape(chunk * rows, width)
        for j in range(width // 128):
            flat[j, pl.ds(pl.multiple_of(i * chunk * rows, 8), chunk * rows), :] = part[:, j * 128:j * 128 + 128]
        return 0

    lax.fori_loop(0, nlat, flatten, 0)

    def take_row(r, to):
        for j in range(width // 128):
            to[r, :, j * 128:j * 128 + 128] = flat[j, pl.ds(r, cols, stride=rows), :].astype(BF)

    same = ((1, 1), (2, 0), (3, 1))
    other = ((0, 1), (1, 0), (2, 1), (3, 0))
    for a, b in zip(same + other, other + same):
        r = (1 - odd) * peer(*a) + odd * peer(*b)
        take_row(r, rowsrc)
        zcopy(r, me).start()
    take_row(me, rowbuf)

    edge = step - step % 16 - 16
    for p in range(nlon):
        at = pl.ds(p * step + edge, 16)
        for h in range(HALF):
            qx[h, at, :] = jnp.zeros((16, 2 * HD), BF)
        for h in range(pairs):
            kx[h, at, :] = jnp.zeros((16, 2 * HD), BF)
            vx[h, at, :] = jnp.zeros((16, 2 * HD), BF)
    gain = gain_ref[...]

    def zbias_stripe(i, _):
        r = i * 32 + lax.broadcasted_iota(jnp.int32, (32, 1), 0)
        c = lax.broadcasted_iota(jnp.int32, (1, span), 1)
        cc = c // step
        cj = c - cc * step
        rc = r // step
        gap = jnp.abs((rc * cols + (r - rc * step)) - (cc * cols + cj))
        circle = jnp.minimum(gap, lon_total - gap).astype(F32) * (1.0 / lon_total)
        dead = cj >= cols
        for h in range(HALF):
            zbias[h, pl.ds(pl.multiple_of(i * 32, 32), 32), :] = jnp.where(dead, FAR, -zs_ref[h] * circle)
        return 0

    lax.fori_loop(0, qb // 32, zbias_stripe, 0)
    group = mbias.shape[2]
    mr = lax.broadcasted_iota(jnp.int32, (group, 1), 0)
    mc = lax.broadcasted_iota(jnp.int32, (1, group), 1)
    mgap = jnp.abs(mr % lat_total - mc % lat_total).astype(F32) * (1.0 / lat_total)
    for h in range(HALF):
        mbias[h // 2, h % 2 * group:(h % 2 + 1) * group] = jnp.where(
            mr // lat_total == mc // lat_total, -ms_ref[h] * mgap, FAR)

    def low(n):
        return lax.broadcasted_iota(jnp.int32, (n, 2 * HD), 1) < HD

    def split_heads(q):
        q = q.astype(BF).astype(F32) * HD ** (-0.5)
        keep = low(q.shape[0])
        return jnp.where(keep, q, 0.0).astype(BF), jnp.where(keep, 0.0, q).astype(BF)

    def project_zonal(x, row):
        n = normed_of(x, gain)
        q = mm(n, wqkv_ref[:, 0:GW])
        k = mm(n, wqkv_ref[:, 2 * GW:3 * GW])
        v = mm(n, wqkv_ref[:, 4 * GW:5 * GW])
        at = pl.ds(pl.multiple_of(row, 64), cols)
        for h in range(pairs):
            w = slice(h * 2 * HD, (h + 1) * 2 * HD)
            qx[2 * h, at, :], qx[2 * h + 1, at, :] = split_heads(q[:, w])
            kx[h, at, :] = k[:, w].astype(BF)
            vx[h, at, :] = v[:, w].astype(BF)

    def project_merid(x, a):
        n = normed_of(x, gain).reshape(chunk * rows, width)
        at = pl.ds(pl.multiple_of(a * rows, 8), rows)
        for i in range(3):
            mqkv[i, :, at, :] = mm(n, wqkv_ref[:, (2 * i + 1) * GW:(2 * i + 2) * GW]).reshape(chunk, rows, GW)

    def take_pieces(first, count):
        def one(i, _):
            slot = i // 2
            p = peer(slot, i % 2)

            @pl.when(p != me)
            def _():
                zcopy(me, p).wait_recv()

            project_zonal(rowbuf[p], slot * qb + lax.rem(p, 2) * step)
            return 0

        lax.fori_loop(first, first + count, one, 0)

    def attend(a, b0, nk, fresh):
        qat = pl.ds(pl.multiple_of(a * qb, 128), qb)
        kat = pl.ds(b0 * qb, nk * qb)
        wide = nk * qb
        turn = [lax.rem(block_of(b0 + i) - block_of(a) + 4, 4) * qb for i in range(nk)]
        for h in range(HALF):
            slot = h % 2
            pr = h // 2
            s = mm_t(qx[h, qat, :], kx[pr, kat, :])
            for i in range(nk):
                s_ref[slot, :, i * qb:(i + 1) * qb] = (
                    s[:, i * qb:(i + 1) * qb] + zbias[h, :, pl.ds(pl.multiple_of(turn[i], 128), qb)])
            for i in range(qb // 32):
                at = slice(i * 32, i * 32 + 32)
                s = s_ref[slot, at, :wide]
                top = jnp.max(s, axis=-1, keepdims=True)
                top = jnp.broadcast_to(top, (32, 2 * HD))
                if not fresh:
                    before = m_ref[a, h, at, :]
                    top = jnp.maximum(top, before)
                    al_ref[h, at, :] = jnp.exp2((before - top) * LOG2E)
                m_ref[a, h, at, :] = top
                e = jnp.exp2((s - jnp.concatenate([top] * (wide // (2 * HD)), axis=1)) * LOG2E)
                lt_ref[h, at, :] = jnp.broadcast_to(jnp.sum(e, axis=-1, keepdims=True), (32, 2 * HD))
                p_ref[slot, at, :wide] = e.astype(BF)
            o_ref[h] = mm(p_ref[slot, :, :wide], vx[pr, kat, :])
        keep = low(qb)
        for pr in range(pairs):
            o = jnp.where(keep, o_ref[2 * pr], o_ref[2 * pr + 1])
            d = jnp.where(keep, lt_ref[2 * pr], lt_ref[2 * pr + 1])
            if not fresh:
                al = jnp.where(keep, al_ref[2 * pr], al_ref[2 * pr + 1])
                o = o + acc[a, pr] * al
                d = d + den[a, pr] * al
            acc[a, pr] = o
            den[a, pr] = d

    def give_back(a):
        o = jnp.concatenate([acc[a, pr] / den[a, pr] for pr in range(pairs)], axis=1).astype(BF)
        for u in range(2):
            dst = block_of(a) * 2 + u
            zout[dst] = o[u * step:u * step + cols]

            @pl.when(dst != me)
            def _():
                zback(dst, me).start()

    def zonal():
        take_pieces(0, 4)

        def near(a, _):
            attend(a, 0, 2, True)
            return 0

        lax.fori_loop(0, 2, near, 0)
        take_pieces(4, 2)
        attend(2, 0, 3, True)

        def far(a, _):
            attend(a, 2, 1, False)
            return 0

        lax.fori_loop(0, 2, far, 0)
        take_pieces(6, 2)

        def last(t, _):
            @pl.when(t == 1)
            def _():
                attend(3, 0, 4, True)

            @pl.when(t != 1)
            def _():
                attend(a_of(t), 3, 1, False)

            give_back(a_of(t))
            return 0

        def a_of(t):
            return jnp.where(t == 0, 2, jnp.where(t == 1, 3, 3 - t))

        lax.fori_loop(0, 4, last, 0)

    gcols = group // lat_total
    batch = batch_of(chunk // gcols)

    def merid():
        def more_merid(k, _):
            a = lax.rem(la + k, nlat)
            mcopy(la, a).wait_recv()
            project_merid(colbuf[a], a)
            return 0

        lax.fori_loop(1, nlat, more_merid, 0)

        def merid_batch(g, _):
            for i in range(batch):
                at = pl.ds((g * batch + i) * gcols, gcols)
                for pr in range(pairs):
                    w = slice(pr * 2 * HD, (pr + 1) * 2 * HD)
                    q = jnp.concatenate(split_heads(mqkv[0, at, :, w].reshape(group, 2 * HD)), axis=0)
                    k = mqkv[1, at, :, w].reshape(group, 2 * HD).astype(BF)
                    ms_scr[i * pairs + pr] = mm_t(q, k) + mbias[pr]
            for i in range(batch * pairs):
                s = ms_scr[i]
                e = jnp.exp2((s - jnp.max(s, axis=-1, keepdims=True)) * LOG2E)
                mp_scr[i] = e.astype(BF)
                ml_scr[i] = jnp.sum(e, axis=-1, keepdims=True)
            keep = low(group)
            for i in range(batch):
                at = pl.ds((g * batch + i) * gcols, gcols)
                outs = []
                for pr in range(pairs):
                    w = slice(pr * 2 * HD, (pr + 1) * 2 * HD)
                    v = mqkv[2, at, :, w].reshape(group, 2 * HD).astype(BF)
                    o = mm(mp_scr[i * pairs + pr], v) / ml_scr[i * pairs + pr]
                    outs.append(jnp.where(keep, o[:group], o[group:]))
                o = jnp.concatenate(outs, axis=1).reshape(gcols, lat_total, GW)
                for a in range(nlat):
                    mout[a, at] = o[:, a * rows:(a + 1) * rows, :].astype(BF)
            return 0

        lax.fori_loop(0, chunk // gcols // batch, merid_batch, 0)
        for k in range(1, nlat):
            mback(lax.rem(la + k, nlat), la).start()

    project_merid(tok_ref[pl.ds(la * chunk, chunk)], la)

    def half(i, _):
        turn = lax.rem(i + odd, 2)

        @pl.when(turn == 0)
        def _():
            zonal()

        @pl.when(turn == 1)
        def _():
            merid()

        return 0

    lax.fori_loop(0, 2, half, 0)
    mret[pl.ds(la * chunk, chunk)] = mout[la]
    zret[me] = zout[me]

    for k in range(1, nlat):
        mback(la, lax.rem(la + k, nlat)).wait_recv()
    out_ref[:, :, GW:2 * GW] = mret[...]

    def finish(i, _):
        t = lax.rem(i, 4)
        s = 2 * t + bit(lax.rem(t, 2), i // 4)

        @pl.when(s != me)
        def _():
            zback(me, s).wait_recv()

        for j in range(GW // 128):
            zflat[j, pl.ds(s, cols, stride=rows), :] = zret[s, :, j * 128:j * 128 + 128].astype(F32)
        return 0

    lax.fori_loop(0, nlon, finish, 0)
    for j in range(GW // 128):
        out_ref[:, :, j * 128:j * 128 + 128] = zflat[j].reshape(cols, rows, 128).astype(BF)

    for k in range(1, nlon):
        p = lax.rem(me + k, nlon)
        zcopy(p, me).wait_send()
        zback(p, me).wait_send()
    for k in range(1, nlat):
        a = lax.rem(la + k, nlat)
        mcopy(a, la).wait_send()
        mback(a, la).wait_send()


def up(n, m):
    return -(-n // m) * m


def exchanged(nlon, nlat, tokens, ln_gain, w_qkv, w_out, zonal_slope, merid_slope):
    rows, cols, width = tokens.shape
    chunk = cols // nlat
    step = up(cols, 64)
    span = nlon * step
    lat_total = nlat * rows
    gcols = max(d for d in range(1, 128 // lat_total + 1) if chunk % d == 0)
    group = gcols * lat_total
    qb = 2 * step
    nblk = nlon // 2
    vm = pl.BlockSpec(memory_space=pltpu.VMEM)
    sm = pl.BlockSpec(memory_space=pltpu.SMEM)
    dma = pltpu.SemaphoreType.DMA
    attended = pl.pallas_call(
        functools.partial(kernel, (nlon, nlat, rows, cols, width)),
        out_shape=jax.ShapeDtypeStruct((cols, rows, width), BF),
        in_specs=[vm, vm, vm, sm, sm],
        out_specs=vm,
        scratch_shapes=[
            pltpu.VMEM((width // 128, cols * rows, 128), F32),
            pltpu.VMEM((nlon, cols, width), BF),
            pltpu.VMEM((nlon, cols, width), BF),
            pltpu.VMEM((nlat, chunk, rows, width), BF),
            pltpu.VMEM((HALF, span, 2 * HD), BF),
            pltpu.VMEM((HALF // 2, span, 2 * HD), BF),
            pltpu.VMEM((HALF // 2, span, 2 * HD), BF),
            pltpu.VMEM((HALF, qb, span), F32),
            pltpu.VMEM((HALF // 2, 2 * group, group), F32),
            pltpu.VMEM((3, chunk, lat_total, GW), F32),
            pltpu.VMEM((2, qb, span), F32),
            pltpu.VMEM((2, qb, span), BF),
            pltpu.VMEM((HALF, qb, 2 * HD), F32),
            pltpu.VMEM((nblk, HALF, qb, 2 * HD), F32),
            pltpu.VMEM((HALF, qb, 2 * HD), F32),
            pltpu.VMEM((HALF, qb, 2 * HD), F32),
            pltpu.VMEM((nblk, HALF // 2, qb, 2 * HD), F32),
            pltpu.VMEM((nblk, HALF // 2, qb, 2 * HD), F32),
            pltpu.VMEM((batch_of(chunk // gcols) * 2, 2 * group, group), F32),
            pltpu.VMEM((batch_of(chunk // gcols) * 2, 2 * group, group), BF),
            pltpu.VMEM((batch_of(chunk // gcols) * 2, 2 * group, 1), F32),
            pltpu.VMEM((nlon, cols, GW), BF),
            pltpu.VMEM((nlat, chunk, rows, GW), BF),
            pltpu.VMEM((nlon, cols, GW), BF),
            pltpu.VMEM((cols, rows, GW), BF),
            pltpu.VMEM((GW // 128, cols * rows, 128), F32),
            dma((nlon,)), dma((nlon,)), dma((nlat,)), dma((nlat,)),
            dma((nlon,)), dma((nlon,)), dma((nlat,)), dma((nlat,)),
        ],
        compiler_params=pltpu.CompilerParams(
            collective_id=0, has_side_effects=True, vmem_limit_bytes=62 * 1024 * 1024),
        name="axial",
    )(jnp.transpose(tokens, (1, 0, 2)), ln_gain.reshape(1, width), w_qkv, zonal_slope, merid_slope)
    update = mm(attended.reshape(cols * rows, width), w_out).astype(BF)
    return jnp.transpose(update.reshape(cols, rows, width), (1, 0, 2))


def solution(mesh):
    nlon, nlat = mesh.shape["lon"], mesh.shape["lat"]

    def body(tokens, *rest):
        rows, cols, _ = tokens.shape
        if rows == 8 == nlon and cols % nlat == 0 and nlat * rows <= 64:
            return exchanged(nlon, nlat, tokens, *rest)
        return gathered(tokens, *rest)

    return jax.shard_map(
        body, mesh=mesh, in_specs=(P("lat", "lon", None), P(), P(), P(), P(), P()),
        out_specs=P("lat", "lon", None), check_vma=False
    )
```

```python
import functools
import math
import jax
import jax.numpy as jnp
from jax import lax
from jax.experimental import pallas as pl
from jax.experimental.pallas import tpu as pltpu
from jax.sharding import PartitionSpec as P

HEADS = 8
HD = 64
HALF = HEADS // 2
GW = HALF * HD
LOG2E = math.log2(math.e)
FAR = -1e30
BF = jnp.bfloat16
F32 = jnp.float32
MESH = pl.DeviceIdType.MESH

def norm_rows(tokens, gain):
    values = tokens.astype(jnp.float32)
    center = values - jnp.mean(values, axis=-1, keepdims=True)
    spread = jnp.mean(center * center, axis=-1, keepdims=True)
    return (center * lax.rsqrt(spread + 1e-05) * gain).astype(jnp.bfloat16)


def fold_step(carry, scores, values, form):
    top, total, summed = carry
    top_new = jnp.maximum(top, jnp.max(scores, axis=-1))
    weights = jnp.exp(scores - top_new[..., None])
    total = jnp.sum(weights, axis=-1)
    summed = jnp.einsum(
        form, weights.astype(jnp.bfloat16), values, preferred_element_type=jnp.float32
    )
    return (top_new, total, summed)


def gathered(tokens, ln_gain, w_qkv, w_out, zonal_slope, merid_slope):
    lat_rows, lon_cols, width = tokens.shape
    half = HEADS // 2
    scale = HD ** (-0.5)
    normed = norm_rows(tokens, ln_gain)
    qkv = jnp.dot(
        normed.reshape(lat_rows * lon_cols, width), w_qkv, preferred_element_type=jnp.float32
    ).astype(jnp.bfloat16)
    qkv = qkv.reshape(lat_rows, lon_cols, 3, 2, half, HD)
    lon_total = lon_cols * lax.axis_size("lon")
    lat_total = lat_rows * lax.axis_size("lat")
    zonal_query = qkv[:, :, 0, 0]
    zonal_pairs = qkv[:, :, 1:, 0]
    query_pos = lax.axis_index("lon") * lon_cols + jnp.arange(lon_cols, dtype=jnp.int32)
    start_carry = (
        jnp.full((lat_rows, half, lon_cols), -1e30, jnp.float32),
        jnp.zeros((lat_rows, half, lon_cols), jnp.float32),
        jnp.zeros((lat_rows, half, lon_cols, HD), jnp.float32),
    )
    piece = lax.all_gather(zonal_pairs, "lon", axis=1, tiled=True)
    count = piece.shape[1]
    key_pos = jnp.arange(count, dtype=jnp.int32)
    gap = jnp.abs(query_pos[:, None] - key_pos[None, :])
    circle = jnp.minimum(gap, lon_total - gap).astype(jnp.float32) / lon_total
    bias = -zonal_slope[:, None, None] * circle[None]
    scores = (
        jnp.einsum(
            "ajhd,akhd->ahjk", zonal_query, piece[:, :, 0], preferred_element_type=jnp.float32
        )
        * scale
        + bias[None]
    )
    top, total, summed = fold_step(start_carry, scores, piece[:, :, 1], "ahjk,akhd->ahjd")
    zonal = jnp.transpose(summed / total[..., None], (0, 2, 1, 3)).reshape(
        lat_rows, lon_cols, half * HD
    )
    merid_query = qkv[:, :, 0, 1]
    merid_pairs = qkv[:, :, 1:, 1]
    row_pos = lax.axis_index("lat") * lat_rows + jnp.arange(lat_rows, dtype=jnp.int32)
    start_carry = (
        jnp.full((lon_cols, half, lat_rows), -1e30, jnp.float32),
        jnp.zeros((lon_cols, half, lat_rows), jnp.float32),
        jnp.zeros((lon_cols, half, lat_rows, HD), jnp.float32),
    )
    piece = lax.all_gather(merid_pairs, "lat", axis=0, tiled=True)
    count = piece.shape[0]
    key_pos = jnp.arange(count, dtype=jnp.int32)
    gap = jnp.abs(row_pos[:, None] - key_pos[None, :]).astype(jnp.float32) / lat_total
    bias = -merid_slope[:, None, None] * gap[None]
    scores = (
        jnp.einsum(
            "ajhd,bjhd->jhab", merid_query, piece[:, :, 0], preferred_element_type=jnp.float32
        )
        * scale
        + bias[None]
    )
    top, total, summed = fold_step(start_carry, scores, piece[:, :, 1], "jhab,bjhd->jhad")
    merid = jnp.transpose(summed / total[..., None], (2, 0, 1, 3)).reshape(
        lat_rows, lon_cols, half * HD
    )
    attended = jnp.concatenate([zonal, merid], axis=-1).astype(jnp.bfloat16)
    update = jnp.dot(
        attended.reshape(lat_rows * lon_cols, width), w_out, preferred_element_type=jnp.float32
    )
    return update.astype(jnp.bfloat16).reshape(lat_rows, lon_cols, width)

def normed_of(x, gain):
    v = x.astype(F32)
    c = v - jnp.mean(v, axis=-1, keepdims=True)
    s = jnp.mean(c * c, axis=-1, keepdims=True)
    return (c * lax.rsqrt(s + 1e-05) * gain).astype(BF)


def mm(a, b):
    return jnp.dot(a, b, preferred_element_type=F32)


def mm_t(a, b):
    return lax.dot_general(a, b, (((1,), (1,)), ((), ())), preferred_element_type=F32)


def batch_of(n):
    return max(d for d in range(1, 6) if n % d == 0)


def kernel(dims, tok_ref, gain_ref, wqkv_ref, zs_ref, ms_ref, out_ref,
           flat, rowsrc, rowbuf, colbuf, qx, kx, vx, zbias, mbias, mqkv, s_ref, p_ref, o_ref,
           m_ref, al_ref, lt_ref, acc, den, ms_scr, mp_scr, ml_scr,
           zout, mout, zret, mret, zflat,
           zsend, zrecv, msend, mrecv, zrs, zrr, mrs, mrr):
    nlon, nlat, rows, cols, width = dims
    chunk = cols // nlat
    step = qx.shape[1] // nlon
    qb = 2 * step
    span = nlon * step
    lon_total = nlon * cols
    lat_total = nlat * rows
    pairs = HALF // 2
    me = lax.axis_index("lon")
    la = lax.axis_index("lat")
    zi = me // 2
    yi = lax.rem(me, 2)
    odd = lax.rem(zi + yi, 2)

    def bit(a, b):
        return a + b - 2 * a * b

    def block_of(slot):
        return 2 * bit(zi // 2, slot // 2) + bit(lax.rem(zi, 2), slot % 2)

    def peer(slot, flip):
        return 2 * block_of(slot) + bit(yi, flip)

    barrier = pltpu.get_barrier_semaphore()
    for k in range(1, nlon):
        pl.semaphore_signal(barrier, inc=1, device_id={"lon": lax.rem(me + k, nlon)}, device_id_type=MESH)
    for k in range(1, nlat):
        pl.semaphore_signal(barrier, inc=1, device_id={"lat": lax.rem(la + k, nlat)}, device_id_type=MESH)
    pl.semaphore_wait(barrier, nlon + nlat - 2)

    def zcopy(dst, src):
        return pltpu.make_async_remote_copy(
            src_ref=rowsrc.at[dst], dst_ref=rowbuf.at[src], send_sem=zsend.at[dst],
            recv_sem=zrecv.at[src], device_id={"lon": dst}, device_id_type=MESH)

    def mcopy(dst, src):
        return pltpu.make_async_remote_copy(
            src_ref=tok_ref.at[pl.ds(dst * chunk, chunk)],
            dst_ref=colbuf.at[src], send_sem=msend.at[dst],
            recv_sem=mrecv.at[src], device_id={"lat": dst}, device_id_type=MESH)

    def zback(dst, src):
        return pltpu.make_async_remote_copy(
            src_ref=zout.at[dst], dst_ref=zret.at[src], send_sem=zrs.at[dst],
            recv_sem=zrr.at[src], device_id={"lon": dst}, device_id_type=MESH)

    def mback(dst, src):
        return pltpu.make_async_remote_copy(
            src_ref=mout.at[dst],
            dst_ref=mret.at[pl.ds(src * chunk, chunk)], send_sem=mrs.at[dst],
            recv_sem=mrr.at[src], device_id={"lat": dst}, device_id_type=MESH)

    for k in range(1, nlat):
        mcopy(lax.rem(la + k, nlat), la).start()

    def flatten(i, _):
        part = tok_ref[pl.ds(i * chunk, chunk)].astype(F32).reshape(chunk * rows, width)
        for j in range(width // 128):
            flat[j, pl.ds(pl.multiple_of(i * chunk * rows, 8), chunk * rows), :] = part[:, j * 128:j * 128 + 128]
        return 0

    lax.fori_loop(0, nlat, flatten, 0)

    def take_row(r, to):
        for j in range(width // 128):
            to[r, :, j * 128:j * 128 + 128] = flat[j, pl.ds(r, cols, stride=rows), :].astype(BF)

    same = ((1, 1), (2, 0), (3, 1))
    other = ((0, 1), (1, 0), (2, 1), (3, 0))
    NEAR = ((0, 1), (1, 0), (1, 1), (2, 0), (2, 1), (3, 0), (3, 1))
    for a, b in zip(NEAR, NEAR):
        r = (1 - odd) * peer(*a) + odd * peer(*b)
        take_row(r, rowsrc)
        zcopy(r, me).start()
    take_row(me, rowbuf)

    edge = step - step % 16 - 16
    for p in range(nlon):
        at = pl.ds(p * step + edge, 16)
        for h in range(HALF):
            qx[h, at, :] = jnp.zeros((16, 2 * HD), BF)
        for h in range(pairs):
            kx[h, at, :] = jnp.zeros((16, 2 * HD), BF)
            vx[h, at, :] = jnp.zeros((16, 2 * HD), BF)
    gain = gain_ref[...]

    def zbias_stripe(i, _):
        r = i * 32 + lax.broadcasted_iota(jnp.int32, (32, 1), 0)
        c = lax.broadcasted_iota(jnp.int32, (1, span), 1)
        cc = c // step
        cj = c - cc * step
        rc = r // step
        gap = jnp.abs((rc * cols + (r - rc * step)) - (cc * cols + cj))
        circle = jnp.minimum(gap, lon_total - gap).astype(F32) * (1.0 / lon_total)
        dead = cj >= cols
        for h in range(HALF):
            zbias[h, pl.ds(pl.multiple_of(i * 32, 32), 32), :] = jnp.where(dead, FAR, -zs_ref[h] * circle)
        return 0

    lax.fori_loop(0, qb // 32, zbias_stripe, 0)
    group = mbias.shape[2]
    mr = lax.broadcasted_iota(jnp.int32, (group, 1), 0)
    mc = lax.broadcasted_iota(jnp.int32, (1, group), 1)
    mgap = jnp.abs(mr % lat_total - mc % lat_total).astype(F32) * (1.0 / lat_total)
    for h in range(HALF):
        mbias[h // 2, h % 2 * group:(h % 2 + 1) * group] = jnp.where(
            mr // lat_total == mc // lat_total, -ms_ref[h] * mgap, FAR)

    def low(n):
        return lax.broadcasted_iota(jnp.int32, (n, 2 * HD), 1) < HD

    def split_heads(q):
        q = q.astype(BF).astype(F32) * HD ** (-0.5)
        keep = low(q.shape[0])
        return jnp.where(keep, q, 0.0).astype(BF), jnp.where(keep, 0.0, q).astype(BF)

    def project_zonal(x, row):
        n = normed_of(x, gain)
        q = mm(n, wqkv_ref[:, 0:GW])
        k = mm(n, wqkv_ref[:, 2 * GW:3 * GW])
        v = mm(n, wqkv_ref[:, 4 * GW:5 * GW])
        at = pl.ds(pl.multiple_of(row, 64), cols)
        for h in range(pairs):
            w = slice(h * 2 * HD, (h + 1) * 2 * HD)
            qx[2 * h, at, :], qx[2 * h + 1, at, :] = split_heads(q[:, w])
            kx[h, at, :] = k[:, w].astype(BF)
            vx[h, at, :] = v[:, w].astype(BF)

    def project_merid(x, a):
        n = normed_of(x, gain).reshape(chunk * rows, width)
        at = pl.ds(pl.multiple_of(a * rows, 8), rows)
        for i in range(3):
            mqkv[i, :, at, :] = mm(n, wqkv_ref[:, (2 * i + 1) * GW:(2 * i + 2) * GW]).reshape(chunk, rows, GW)

    def take_pieces(first, count):
        def one(i, _):
            slot = i // 2
            p = peer(slot, i % 2)

            @pl.when(p != me)
            def _():
                zcopy(me, p).wait_recv()

            project_zonal(rowbuf[p], slot * qb + lax.rem(p, 2) * step)
            return 0

        lax.fori_loop(first, first + count, one, 0)

    def attend(a, b0, nk, fresh):
        qat = pl.ds(pl.multiple_of(a * qb, 128), qb)
        kat = pl.ds(b0 * qb, nk * qb)
        wide = nk * qb
        turn = [lax.rem(block_of(b0 + i) - block_of(a) + 4, 4) * qb for i in range(nk)]
        for h in range(HALF):
            slot = h % 2
            pr = h // 2
            s = mm_t(qx[h, qat, :], kx[pr, kat, :])
            for i in range(nk):
                s_ref[slot, :, i * qb:(i + 1) * qb] = (
                    s[:, i * qb:(i + 1) * qb] + zbias[h, :, pl.ds(pl.multiple_of(turn[i], 128), qb)])
            for i in range(qb // 32):
                at = slice(i * 32, i * 32 + 32)
                s = s_ref[slot, at, :wide]
                top = jnp.max(s, axis=-1, keepdims=True)
                top = jnp.broadcast_to(top, (32, 2 * HD))
                if not fresh:
                    before = m_ref[a, h, at, :]
                    top = jnp.maximum(top, before)
                    al_ref[h, at, :] = jnp.exp2((before - top) * LOG2E)
                m_ref[a, h, at, :] = top
                e = jnp.exp2((s - jnp.concatenate([top] * (wide // (2 * HD)), axis=1)) * LOG2E)
                lt_ref[h, at, :] = jnp.broadcast_to(jnp.sum(e, axis=-1, keepdims=True), (32, 2 * HD))
                p_ref[slot, at, :wide] = e.astype(BF)
            o_ref[h] = mm(p_ref[slot, :, :wide], vx[pr, kat, :])
        keep = low(qb)
        for pr in range(pairs):
            o = jnp.where(keep, o_ref[2 * pr], o_ref[2 * pr + 1])
            d = jnp.where(keep, lt_ref[2 * pr], lt_ref[2 * pr + 1])
            if not fresh:
                al = jnp.where(keep, al_ref[2 * pr], al_ref[2 * pr + 1])
                o = o + acc[a, pr] * al
                d = d + den[a, pr] * al
            acc[a, pr] = o
            den[a, pr] = d

    def give_back(a):
        o = jnp.concatenate([acc[a, pr] / den[a, pr] for pr in range(pairs)], axis=1).astype(BF)
        for u in range(2):
            dst = block_of(a) * 2 + u
            zout[dst] = o[u * step:u * step + cols]

            @pl.when(dst != me)
            def _():
                zback(dst, me).start()

    def zonal():
        take_pieces(0, 4)

        def near(a, _):
            attend(a, 0, 2, True)
            return 0

        lax.fori_loop(0, 2, near, 0)
        take_pieces(4, 2)
        attend(2, 0, 3, True)

        def far(a, _):
            attend(a, 2, 1, False)
            return 0

        lax.fori_loop(0, 2, far, 0)
        take_pieces(6, 2)

        def last(t, _):
            @pl.when(t == 1)
            def _():
                attend(3, 0, 4, True)

            @pl.when(t != 1)
            def _():
                attend(a_of(t), 3, 1, False)

            give_back(a_of(t))
            return 0

        def a_of(t):
            return jnp.where(t == 0, 2, jnp.where(t == 1, 3, 3 - t))

        lax.fori_loop(0, 4, last, 0)

    gcols = group // lat_total
    batch = batch_of(chunk // gcols)

    def merid():
        def more_merid(k, _):
            a = lax.rem(la + k, nlat)
            mcopy(la, a).wait_recv()
            project_merid(colbuf[a], a)
            return 0

        lax.fori_loop(1, nlat, more_merid, 0)

        def merid_batch(g, _):
            for i in range(batch):
                at = pl.ds((g * batch + i) * gcols, gcols)
                for pr in range(pairs):
                    w = slice(pr * 2 * HD, (pr + 1) * 2 * HD)
                    q = jnp.concatenate(split_heads(mqkv[0, at, :, w].reshape(group, 2 * HD)), axis=0)
                    k = mqkv[1, at, :, w].reshape(group, 2 * HD).astype(BF)
                    ms_scr[i * pairs + pr] = mm_t(q, k) + mbias[pr]
            for i in range(batch * pairs):
                s = ms_scr[i]
                e = jnp.exp2((s - jnp.max(s, axis=-1, keepdims=True)) * LOG2E)
                mp_scr[i] = e.astype(BF)
                ml_scr[i] = jnp.sum(e, axis=-1, keepdims=True)
            keep = low(group)
            for i in range(batch):
                at = pl.ds((g * batch + i) * gcols, gcols)
                outs = []
                for pr in range(pairs):
                    w = slice(pr * 2 * HD, (pr + 1) * 2 * HD)
                    v = mqkv[2, at, :, w].reshape(group, 2 * HD).astype(BF)
                    o = mm(mp_scr[i * pairs + pr], v) / ml_scr[i * pairs + pr]
                    outs.append(jnp.where(keep, o[:group], o[group:]))
                o = jnp.concatenate(outs, axis=1).reshape(gcols, lat_total, GW)
                for a in range(nlat):
                    mout[a, at] = o[:, a * rows:(a + 1) * rows, :].astype(BF)
            return 0

        lax.fori_loop(0, chunk // gcols // batch, merid_batch, 0)
        for k in range(1, nlat):
            mback(lax.rem(la + k, nlat), la).start()

    project_merid(tok_ref[pl.ds(la * chunk, chunk)], la)

    def half(i, _):
        turn = lax.rem(i + 1, 2)

        @pl.when(turn == 0)
        def _():
            zonal()

        @pl.when(turn == 1)
        def _():
            merid()

        return 0

    lax.fori_loop(0, 2, half, 0)
    mret[pl.ds(la * chunk, chunk)] = mout[la]
    zret[me] = zout[me]

    for k in range(1, nlat):
        mback(la, lax.rem(la + k, nlat)).wait_recv()
    out_ref[:, :, GW:2 * GW] = mret[...]

    def finish(i, _):
        t = lax.rem(i, 4)
        s = 2 * t + bit(lax.rem(t, 2), i // 4)

        @pl.when(s != me)
        def _():
            zback(me, s).wait_recv()

        for j in range(GW // 128):
            zflat[j, pl.ds(s, cols, stride=rows), :] = zret[s, :, j * 128:j * 128 + 128].astype(F32)
        return 0

    lax.fori_loop(0, nlon, finish, 0)
    for j in range(GW // 128):
        out_ref[:, :, j * 128:j * 128 + 128] = zflat[j].reshape(cols, rows, 128).astype(BF)

    for k in range(1, nlon):
        p = lax.rem(me + k, nlon)
        zcopy(p, me).wait_send()
        zback(p, me).wait_send()
    for k in range(1, nlat):
        a = lax.rem(la + k, nlat)
        mcopy(a, la).wait_send()
        mback(a, la).wait_send()


def up(n, m):
    return -(-n // m) * m


def exchanged(nlon, nlat, tokens, ln_gain, w_qkv, w_out, zonal_slope, merid_slope):
    rows, cols, width = tokens.shape
    chunk = cols // nlat
    step = up(cols, 64)
    span = nlon * step
    lat_total = nlat * rows
    gcols = max(d for d in range(1, 128 // lat_total + 1) if chunk % d == 0)
    group = gcols * lat_total
    qb = 2 * step
    nblk = nlon // 2
    vm = pl.BlockSpec(memory_space=pltpu.VMEM)
    sm = pl.BlockSpec(memory_space=pltpu.SMEM)
    dma = pltpu.SemaphoreType.DMA
    attended = pl.pallas_call(
        functools.partial(kernel, (nlon, nlat, rows, cols, width)),
        out_shape=jax.ShapeDtypeStruct((cols, rows, width), BF),
        in_specs=[vm, vm, vm, sm, sm],
        out_specs=vm,
        scratch_shapes=[
            pltpu.VMEM((width // 128, cols * rows, 128), F32),
            pltpu.VMEM((nlon, cols, width), BF),
            pltpu.VMEM((nlon, cols, width), BF),
            pltpu.VMEM((nlat, chunk, rows, width), BF),
            pltpu.VMEM((HALF, span, 2 * HD), BF),
            pltpu.VMEM((HALF // 2, span, 2 * HD), BF),
            pltpu.VMEM((HALF // 2, span, 2 * HD), BF),
            pltpu.VMEM((HALF, qb, span), F32),
            pltpu.VMEM((HALF // 2, 2 * group, group), F32),
            pltpu.VMEM((3, chunk, lat_total, GW), F32),
            pltpu.VMEM((2, qb, span), F32),
            pltpu.VMEM((2, qb, span), BF),
            pltpu.VMEM((HALF, qb, 2 * HD), F32),
            pltpu.VMEM((nblk, HALF, qb, 2 * HD), F32),
            pltpu.VMEM((HALF, qb, 2 * HD), F32),
            pltpu.VMEM((HALF, qb, 2 * HD), F32),
            pltpu.VMEM((nblk, HALF // 2, qb, 2 * HD), F32),
            pltpu.VMEM((nblk, HALF // 2, qb, 2 * HD), F32),
            pltpu.VMEM((batch_of(chunk // gcols) * 2, 2 * group, group), F32),
            pltpu.VMEM((batch_of(chunk // gcols) * 2, 2 * group, group), BF),
            pltpu.VMEM((batch_of(chunk // gcols) * 2, 2 * group, 1), F32),
            pltpu.VMEM((nlon, cols, GW), BF),
            pltpu.VMEM((nlat, chunk, rows, GW), BF),
            pltpu.VMEM((nlon, cols, GW), BF),
            pltpu.VMEM((cols, rows, GW), BF),
            pltpu.VMEM((GW // 128, cols * rows, 128), F32),
            dma((nlon,)), dma((nlon,)), dma((nlat,)), dma((nlat,)),
            dma((nlon,)), dma((nlon,)), dma((nlat,)), dma((nlat,)),
        ],
        compiler_params=pltpu.CompilerParams(
            collective_id=0, has_side_effects=True, vmem_limit_bytes=62 * 1024 * 1024),
        name="axial",
    )(jnp.transpose(tokens, (1, 0, 2)), ln_gain.reshape(1, width), w_qkv, zonal_slope, merid_slope)
    update = mm(attended.reshape(cols * rows, width), w_out).astype(BF)
    return jnp.transpose(update.reshape(cols, rows, width), (1, 0, 2))


def solution(mesh):
    nlon, nlat = mesh.shape["lon"], mesh.shape["lat"]

    def body(tokens, *rest):
        rows, cols, _ = tokens.shape
        if rows == 8 == nlon and cols % nlat == 0 and nlat * rows <= 64:
            return exchanged(nlon, nlat, tokens, *rest)
        return gathered(tokens, *rest)

    return jax.shard_map(
        body, mesh=mesh, in_specs=(P("lat", "lon", None), P(), P(), P(), P(), P()),
        out_specs=P("lat", "lon", None), check_vma=False
    )
```

```python
import functools
import math
import jax
import jax.numpy as jnp
from jax import lax
from jax.experimental import pallas as pl
from jax.experimental.pallas import tpu as pltpu
from jax.sharding import PartitionSpec as P

HEADS = 8
HD = 64
HALF = HEADS // 2
GW = HALF * HD
LOG2E = math.log2(math.e)
FAR = -1e30
BF = jnp.bfloat16
F32 = jnp.float32
MESH = pl.DeviceIdType.MESH

def norm_rows(tokens, gain):
    values = tokens.astype(jnp.float32)
    center = values - jnp.mean(values, axis=-1, keepdims=True)
    spread = jnp.mean(center * center, axis=-1, keepdims=True)
    return (center * lax.rsqrt(spread + 1e-05) * gain).astype(jnp.bfloat16)


def fold_step(carry, scores, values, form):
    top, total, summed = carry
    top_new = jnp.maximum(top, jnp.max(scores, axis=-1))
    weights = jnp.exp(scores - top_new[..., None])
    total = jnp.sum(weights, axis=-1)
    summed = jnp.einsum(
        form, weights.astype(jnp.bfloat16), values, preferred_element_type=jnp.float32
    )
    return (top_new, total, summed)


def gathered(tokens, ln_gain, w_qkv, w_out, zonal_slope, merid_slope):
    lat_rows, lon_cols, width = tokens.shape
    half = HEADS // 2
    scale = HD ** (-0.5)
    normed = norm_rows(tokens, ln_gain)
    qkv = jnp.dot(
        normed.reshape(lat_rows * lon_cols, width), w_qkv, preferred_element_type=jnp.float32
    ).astype(jnp.bfloat16)
    qkv = qkv.reshape(lat_rows, lon_cols, 3, 2, half, HD)
    lon_total = lon_cols * lax.axis_size("lon")
    lat_total = lat_rows * lax.axis_size("lat")
    zonal_query = qkv[:, :, 0, 0]
    zonal_pairs = qkv[:, :, 1:, 0]
    query_pos = lax.axis_index("lon") * lon_cols + jnp.arange(lon_cols, dtype=jnp.int32)
    start_carry = (
        jnp.full((lat_rows, half, lon_cols), -1e30, jnp.float32),
        jnp.zeros((lat_rows, half, lon_cols), jnp.float32),
        jnp.zeros((lat_rows, half, lon_cols, HD), jnp.float32),
    )
    piece = lax.all_gather(zonal_pairs, "lon", axis=1, tiled=True)
    count = piece.shape[1]
    key_pos = jnp.arange(count, dtype=jnp.int32)
    gap = jnp.abs(query_pos[:, None] - key_pos[None, :])
    circle = jnp.minimum(gap, lon_total - gap).astype(jnp.float32) / lon_total
    bias = -zonal_slope[:, None, None] * circle[None]
    scores = (
        jnp.einsum(
            "ajhd,akhd->ahjk", zonal_query, piece[:, :, 0], preferred_element_type=jnp.float32
        )
        * scale
        + bias[None]
    )
    top, total, summed = fold_step(start_carry, scores, piece[:, :, 1], "ahjk,akhd->ahjd")
    zonal = jnp.transpose(summed / total[..., None], (0, 2, 1, 3)).reshape(
        lat_rows, lon_cols, half * HD
    )
    merid_query = qkv[:, :, 0, 1]
    merid_pairs = qkv[:, :, 1:, 1]
    row_pos = lax.axis_index("lat") * lat_rows + jnp.arange(lat_rows, dtype=jnp.int32)
    start_carry = (
        jnp.full((lon_cols, half, lat_rows), -1e30, jnp.float32),
        jnp.zeros((lon_cols, half, lat_rows), jnp.float32),
        jnp.zeros((lon_cols, half, lat_rows, HD), jnp.float32),
    )
    piece = lax.all_gather(merid_pairs, "lat", axis=0, tiled=True)
    count = piece.shape[0]
    key_pos = jnp.arange(count, dtype=jnp.int32)
    gap = jnp.abs(row_pos[:, None] - key_pos[None, :]).astype(jnp.float32) / lat_total
    bias = -merid_slope[:, None, None] * gap[None]
    scores = (
        jnp.einsum(
            "ajhd,bjhd->jhab", merid_query, piece[:, :, 0], preferred_element_type=jnp.float32
        )
        * scale
        + bias[None]
    )
    top, total, summed = fold_step(start_carry, scores, piece[:, :, 1], "jhab,bjhd->jhad")
    merid = jnp.transpose(summed / total[..., None], (2, 0, 1, 3)).reshape(
        lat_rows, lon_cols, half * HD
    )
    attended = jnp.concatenate([zonal, merid], axis=-1).astype(jnp.bfloat16)
    update = jnp.dot(
        attended.reshape(lat_rows * lon_cols, width), w_out, preferred_element_type=jnp.float32
    )
    return update.astype(jnp.bfloat16).reshape(lat_rows, lon_cols, width)

def normed_of(x, gain):
    v = x.astype(F32)
    c = v - jnp.mean(v, axis=-1, keepdims=True)
    s = jnp.mean(c * c, axis=-1, keepdims=True)
    return (c * lax.rsqrt(s + 1e-05) * gain).astype(BF)


def mm(a, b):
    return jnp.dot(a, b, preferred_element_type=F32)


def mm_t(a, b):
    return lax.dot_general(a, b, (((1,), (1,)), ((), ())), preferred_element_type=F32)


def batch_of(n):
    return max(d for d in range(1, 6) if n % d == 0)


def kernel(dims, tok_ref, gain_ref, wqkv_ref, zs_ref, ms_ref, out_ref,
           flat, rowsrc, rowbuf, colbuf, qx, kx, vx, zbias, mbias, mqkv, s_ref, p_ref, o_ref,
           m_ref, al_ref, lt_ref, acc, den, ms_scr, mp_scr, ml_scr,
           zout, mout, zret, mret, zflat,
           zsend, zrecv, msend, mrecv, zrs, zrr, mrs, mrr):
    nlon, nlat, rows, cols, width = dims
    chunk = cols // nlat
    step = qx.shape[1] // nlon
    qb = 2 * step
    span = nlon * step
    lon_total = nlon * cols
    lat_total = nlat * rows
    pairs = HALF // 2
    me = lax.axis_index("lon")
    la = lax.axis_index("lat")
    zi = me // 2
    yi = lax.rem(me, 2)
    odd = lax.rem(zi + yi, 2)

    def bit(a, b):
        return a + b - 2 * a * b

    def block_of(slot):
        return 2 * bit(zi // 2, slot // 2) + bit(lax.rem(zi, 2), slot % 2)

    def peer(slot, flip):
        return 2 * block_of(slot) + bit(yi, flip)

    barrier = pltpu.get_barrier_semaphore()
    for k in range(1, nlon):
        pl.semaphore_signal(barrier, inc=1, device_id={"lon": lax.rem(me + k, nlon)}, device_id_type=MESH)
    for k in range(1, nlat):
        pl.semaphore_signal(barrier, inc=1, device_id={"lat": lax.rem(la + k, nlat)}, device_id_type=MESH)
    pl.semaphore_wait(barrier, nlon + nlat - 2)

    def zcopy(dst, src):
        return pltpu.make_async_remote_copy(
            src_ref=rowsrc.at[dst], dst_ref=rowbuf.at[src], send_sem=zsend.at[dst],
            recv_sem=zrecv.at[src], device_id={"lon": dst}, device_id_type=MESH)

    def mcopy(dst, src):
        return pltpu.make_async_remote_copy(
            src_ref=tok_ref.at[pl.ds(dst * chunk, chunk)],
            dst_ref=colbuf.at[src], send_sem=msend.at[dst],
            recv_sem=mrecv.at[src], device_id={"lat": dst}, device_id_type=MESH)

    def zback(dst, src):
        return pltpu.make_async_remote_copy(
            src_ref=zout.at[dst], dst_ref=zret.at[src], send_sem=zrs.at[dst],
            recv_sem=zrr.at[src], device_id={"lon": dst}, device_id_type=MESH)

    def mback(dst, src):
        return pltpu.make_async_remote_copy(
            src_ref=mout.at[dst],
            dst_ref=mret.at[pl.ds(src * chunk, chunk)], send_sem=mrs.at[dst],
            recv_sem=mrr.at[src], device_id={"lat": dst}, device_id_type=MESH)

    for k in range(1, nlat):
        mcopy(lax.rem(la + k, nlat), la).start()

    def flatten(i, _):
        part = tok_ref[pl.ds(i * chunk, chunk)].astype(F32).reshape(chunk * rows, width)
        for j in range(width // 128):
            flat[j, pl.ds(pl.multiple_of(i * chunk * rows, 8), chunk * rows), :] = part[:, j * 128:j * 128 + 128]
        return 0

    lax.fori_loop(0, nlat, flatten, 0)

    def take_row(r, to):
        for j in range(width // 128):
            to[r, :, j * 128:j * 128 + 128] = flat[j, pl.ds(r, cols, stride=rows), :].astype(BF)

    same = ((1, 1), (2, 0), (3, 1))
    other = ((0, 1), (1, 0), (2, 1), (3, 0))
    NEAR = ((0, 1), (1, 0), (1, 1), (2, 0), (2, 1), (3, 0), (3, 1))
    for a, b in zip(NEAR, NEAR):
        r = (1 - odd) * peer(*a) + odd * peer(*b)
        take_row(r, rowsrc)
        zcopy(r, me).start()
    take_row(me, rowbuf)

    edge = step - step % 16 - 16
    for p in range(nlon):
        at = pl.ds(p * step + edge, 16)
        for h in range(HALF):
            qx[h, at, :] = jnp.zeros((16, 2 * HD), BF)
        for h in range(pairs):
            kx[h, at, :] = jnp.zeros((16, 2 * HD), BF)
            vx[h, at, :] = jnp.zeros((16, 2 * HD), BF)
    gain = gain_ref[...]

    def zbias_stripe(i, _):
        r = i * 32 + lax.broadcasted_iota(jnp.int32, (32, 1), 0)
        c = lax.broadcasted_iota(jnp.int32, (1, span), 1)
        cc = c // step
        cj = c - cc * step
        rc = r // step
        gap = jnp.abs((rc * cols + (r - rc * step)) - (cc * cols + cj))
        circle = jnp.minimum(gap, lon_total - gap).astype(F32) * (1.0 / lon_total)
        dead = cj >= cols
        for h in range(HALF):
            zbias[h, pl.ds(pl.multiple_of(i * 32, 32), 32), :] = jnp.where(dead, FAR, -zs_ref[h] * circle)
        return 0

    lax.fori_loop(0, qb // 32, zbias_stripe, 0)
    group = mbias.shape[2]
    mr = lax.broadcasted_iota(jnp.int32, (group, 1), 0)
    mc = lax.broadcasted_iota(jnp.int32, (1, group), 1)
    mgap = jnp.abs(mr % lat_total - mc % lat_total).astype(F32) * (1.0 / lat_total)
    for h in range(HALF):
        mbias[h // 2, h % 2 * group:(h % 2 + 1) * group] = jnp.where(
            mr // lat_total == mc // lat_total, -ms_ref[h] * mgap, FAR)

    def low(n):
        return lax.broadcasted_iota(jnp.int32, (n, 2 * HD), 1) < HD

    def split_heads(q):
        q = q.astype(BF).astype(F32) * HD ** (-0.5)
        keep = low(q.shape[0])
        return jnp.where(keep, q, 0.0).astype(BF), jnp.where(keep, 0.0, q).astype(BF)

    def project_zonal(x, row):
        n = normed_of(x, gain)
        q = mm(n, wqkv_ref[:, 0:GW])
        k = mm(n, wqkv_ref[:, 2 * GW:3 * GW])
        v = mm(n, wqkv_ref[:, 4 * GW:5 * GW])
        at = pl.ds(pl.multiple_of(row, 64), cols)
        for h in range(pairs):
            w = slice(h * 2 * HD, (h + 1) * 2 * HD)
            qx[2 * h, at, :], qx[2 * h + 1, at, :] = split_heads(q[:, w])
            kx[h, at, :] = k[:, w].astype(BF)
            vx[h, at, :] = v[:, w].astype(BF)

    def project_merid(x, a):
        n = normed_of(x, gain).reshape(chunk * rows, width)
        at = pl.ds(pl.multiple_of(a * rows, 8), rows)
        for i in range(3):
            mqkv[i, :, at, :] = mm(n, wqkv_ref[:, (2 * i + 1) * GW:(2 * i + 2) * GW]).reshape(chunk, rows, GW)

    def take_pieces(first, count):
        def one(i, _):
            slot = i // 2
            p = peer(slot, i % 2)

            @pl.when(p != me)
            def _():
                zcopy(me, p).wait_recv()

            project_zonal(rowbuf[p], slot * qb + lax.rem(p, 2) * step)
            return 0

        lax.fori_loop(first, first + count, one, 0)

    def attend(a, b0, nk, fresh):
        qat = pl.ds(pl.multiple_of(a * qb, 128), qb)
        kat = pl.ds(b0 * qb, nk * qb)
        wide = nk * qb
        turn = [lax.rem(block_of(b0 + i) - block_of(a) + 4, 4) * qb for i in range(nk)]
        for h in range(HALF):
            slot = h % 2
            pr = h // 2
            s = mm_t(qx[h, qat, :], kx[pr, kat, :])
            for i in range(nk):
                s_ref[slot, :, i * qb:(i + 1) * qb] = (
                    s[:, i * qb:(i + 1) * qb] + zbias[h, :, pl.ds(pl.multiple_of(turn[i], 128), qb)])
            for i in range(qb // 32):
                at = slice(i * 32, i * 32 + 32)
                s = s_ref[slot, at, :wide]
                top = jnp.max(s, axis=-1, keepdims=True)
                top = jnp.broadcast_to(top, (32, 2 * HD))
                if not fresh:
                    before = m_ref[a, h, at, :]
                    top = jnp.maximum(top, before)
                    al_ref[h, at, :] = jnp.exp2((before - top) * LOG2E)
                m_ref[a, h, at, :] = top
                e = jnp.exp2((s - jnp.concatenate([top] * (wide // (2 * HD)), axis=1)) * LOG2E)
                lt_ref[h, at, :] = jnp.broadcast_to(jnp.sum(e, axis=-1, keepdims=True), (32, 2 * HD))
                p_ref[slot, at, :wide] = e.astype(BF)
            o_ref[h] = mm(p_ref[slot, :, :wide], vx[pr, kat, :])
        keep = low(qb)
        for pr in range(pairs):
            o = jnp.where(keep, o_ref[2 * pr], o_ref[2 * pr + 1])
            d = jnp.where(keep, lt_ref[2 * pr], lt_ref[2 * pr + 1])
            if not fresh:
                al = jnp.where(keep, al_ref[2 * pr], al_ref[2 * pr + 1])
                o = o + acc[a, pr] * al
                d = d + den[a, pr] * al
            acc[a, pr] = o
            den[a, pr] = d

    def give_back(a):
        o = jnp.concatenate([acc[a, pr] / den[a, pr] for pr in range(pairs)], axis=1).astype(BF)
        for u in range(2):
            dst = block_of(a) * 2 + u
            zout[dst] = o[u * step:u * step + cols]

            @pl.when(dst != me)
            def _():
                zback(dst, me).start()

    def zonal_near():
        take_pieces(0, 4)

        def near(a, _):
            attend(a, 0, 2, True)
            return 0

        lax.fori_loop(0, 2, near, 0)

    def zonal_far():
        take_pieces(4, 2)
        attend(2, 0, 3, True)

        def far(a, _):
            attend(a, 2, 1, False)
            return 0

        lax.fori_loop(0, 2, far, 0)
        take_pieces(6, 2)

        def last(t, _):
            @pl.when(t == 1)
            def _():
                attend(3, 0, 4, True)

            @pl.when(t != 1)
            def _():
                attend(a_of(t), 3, 1, False)

            give_back(a_of(t))
            return 0

        def a_of(t):
            return jnp.where(t == 0, 2, jnp.where(t == 1, 3, 3 - t))

        lax.fori_loop(0, 4, last, 0)

    gcols = group // lat_total
    batch = batch_of(chunk // gcols)

    def merid():
        def more_merid(k, _):
            a = lax.rem(la + k, nlat)
            mcopy(la, a).wait_recv()
            project_merid(colbuf[a], a)
            return 0

        lax.fori_loop(1, nlat, more_merid, 0)

        def merid_batch(g, _):
            for i in range(batch):
                at = pl.ds((g * batch + i) * gcols, gcols)
                for pr in range(pairs):
                    w = slice(pr * 2 * HD, (pr + 1) * 2 * HD)
                    q = jnp.concatenate(split_heads(mqkv[0, at, :, w].reshape(group, 2 * HD)), axis=0)
                    k = mqkv[1, at, :, w].reshape(group, 2 * HD).astype(BF)
                    ms_scr[i * pairs + pr] = mm_t(q, k) + mbias[pr]
            for i in range(batch * pairs):
                s = ms_scr[i]
                e = jnp.exp2((s - jnp.max(s, axis=-1, keepdims=True)) * LOG2E)
                mp_scr[i] = e.astype(BF)
                ml_scr[i] = jnp.sum(e, axis=-1, keepdims=True)
            keep = low(group)
            for i in range(batch):
                at = pl.ds((g * batch + i) * gcols, gcols)
                outs = []
                for pr in range(pairs):
                    w = slice(pr * 2 * HD, (pr + 1) * 2 * HD)
                    v = mqkv[2, at, :, w].reshape(group, 2 * HD).astype(BF)
                    o = mm(mp_scr[i * pairs + pr], v) / ml_scr[i * pairs + pr]
                    outs.append(jnp.where(keep, o[:group], o[group:]))
                o = jnp.concatenate(outs, axis=1).reshape(gcols, lat_total, GW)
                for a in range(nlat):
                    mout[a, at] = o[:, a * rows:(a + 1) * rows, :].astype(BF)
            return 0

        lax.fori_loop(0, chunk // gcols // batch, merid_batch, 0)
        for k in range(1, nlat):
            mback(lax.rem(la + k, nlat), la).start()

    project_merid(tok_ref[pl.ds(la * chunk, chunk)], la)

    zonal_near()
    merid()
    zonal_far()
    mret[pl.ds(la * chunk, chunk)] = mout[la]
    zret[me] = zout[me]

    for k in range(1, nlat):
        mback(la, lax.rem(la + k, nlat)).wait_recv()
    out_ref[:, :, GW:2 * GW] = mret[...]

    def finish(i, _):
        t = i // 2
        s = peer(jnp.where(t < 2, 2 + t, 3 - t), i % 2)

        @pl.when(s != me)
        def _():
            zback(me, s).wait_recv()

        for j in range(GW // 128):
            zflat[j, pl.ds(s, cols, stride=rows), :] = zret[s, :, j * 128:j * 128 + 128].astype(F32)
        return 0

    lax.fori_loop(0, nlon, finish, 0)
    for j in range(GW // 128):
        out_ref[:, :, j * 128:j * 128 + 128] = zflat[j].reshape(cols, rows, 128).astype(BF)

    for k in range(1, nlon):
        p = lax.rem(me + k, nlon)
        zcopy(p, me).wait_send()
        zback(p, me).wait_send()
    for k in range(1, nlat):
        a = lax.rem(la + k, nlat)
        mcopy(a, la).wait_send()
        mback(a, la).wait_send()


def up(n, m):
    return -(-n // m) * m


def exchanged(nlon, nlat, tokens, ln_gain, w_qkv, w_out, zonal_slope, merid_slope):
    rows, cols, width = tokens.shape
    chunk = cols // nlat
    step = up(cols, 64)
    span = nlon * step
    lat_total = nlat * rows
    gcols = max(d for d in range(1, 128 // lat_total + 1) if chunk % d == 0)
    group = gcols * lat_total
    qb = 2 * step
    nblk = nlon // 2
    vm = pl.BlockSpec(memory_space=pltpu.VMEM)
    sm = pl.BlockSpec(memory_space=pltpu.SMEM)
    dma = pltpu.SemaphoreType.DMA
    attended = pl.pallas_call(
        functools.partial(kernel, (nlon, nlat, rows, cols, width)),
        out_shape=jax.ShapeDtypeStruct((cols, rows, width), BF),
        in_specs=[vm, vm, vm, sm, sm],
        out_specs=vm,
        scratch_shapes=[
            pltpu.VMEM((width // 128, cols * rows, 128), F32),
            pltpu.VMEM((nlon, cols, width), BF),
            pltpu.VMEM((nlon, cols, width), BF),
            pltpu.VMEM((nlat, chunk, rows, width), BF),
            pltpu.VMEM((HALF, span, 2 * HD), BF),
            pltpu.VMEM((HALF // 2, span, 2 * HD), BF),
            pltpu.VMEM((HALF // 2, span, 2 * HD), BF),
            pltpu.VMEM((HALF, qb, span), F32),
            pltpu.VMEM((HALF // 2, 2 * group, group), F32),
            pltpu.VMEM((3, chunk, lat_total, GW), F32),
            pltpu.VMEM((2, qb, span), F32),
            pltpu.VMEM((2, qb, span), BF),
            pltpu.VMEM((HALF, qb, 2 * HD), F32),
            pltpu.VMEM((nblk, HALF, qb, 2 * HD), F32),
            pltpu.VMEM((HALF, qb, 2 * HD), F32),
            pltpu.VMEM((HALF, qb, 2 * HD), F32),
            pltpu.VMEM((nblk, HALF // 2, qb, 2 * HD), F32),
            pltpu.VMEM((nblk, HALF // 2, qb, 2 * HD), F32),
            pltpu.VMEM((batch_of(chunk // gcols) * 2, 2 * group, group), F32),
            pltpu.VMEM((batch_of(chunk // gcols) * 2, 2 * group, group), BF),
            pltpu.VMEM((batch_of(chunk // gcols) * 2, 2 * group, 1), F32),
            pltpu.VMEM((nlon, cols, GW), BF),
            pltpu.VMEM((nlat, chunk, rows, GW), BF),
            pltpu.VMEM((nlon, cols, GW), BF),
            pltpu.VMEM((cols, rows, GW), BF),
            pltpu.VMEM((GW // 128, cols * rows, 128), F32),
            dma((nlon,)), dma((nlon,)), dma((nlat,)), dma((nlat,)),
            dma((nlon,)), dma((nlon,)), dma((nlat,)), dma((nlat,)),
        ],
        compiler_params=pltpu.CompilerParams(
            collective_id=0, has_side_effects=True, vmem_limit_bytes=62 * 1024 * 1024),
        name="axial",
    )(jnp.transpose(tokens, (1, 0, 2)), ln_gain.reshape(1, width), w_qkv, zonal_slope, merid_slope)
    update = mm(attended.reshape(cols * rows, width), w_out).astype(BF)
    return jnp.transpose(update.reshape(cols, rows, width), (1, 0, 2))


def solution(mesh):
    nlon, nlat = mesh.shape["lon"], mesh.shape["lat"]

    def body(tokens, *rest):
        rows, cols, _ = tokens.shape
        if rows == 8 == nlon and cols % nlat == 0 and nlat * rows <= 64:
            return exchanged(nlon, nlat, tokens, *rest)
        return gathered(tokens, *rest)

    return jax.shard_map(
        body, mesh=mesh, in_specs=(P("lat", "lon", None), P(), P(), P(), P(), P()),
        out_specs=P("lat", "lon", None), check_vma=False
    )
```
